32 devices in a mesh: design: 2 (over y), space: 8 (over z, x), case: 2 (over core).
Axes of the slice: x: 2, y: 2, z: 4, core: 2. Of those that a mesh axis runs over, the one named last changes fastest.
Arguments:
- displacement: float32 [16, 3, 96, 16, 128], P(('design', 'case'), None, 'space'), parts along dimension 0, may hold values from -3 to 3
- forces: float32 [16, 3, 96, 16, 128], P(('design', 'case'), None, 'space'), parts along dimension 0, may hold values from -13.6 to 13.6
- density: float32 [192, 16, 128], P(('design', 'space')), parts along dimension 0, may hold values from 0.1 to 1
- support_mask: int32 [192, 16, 128], P(('design', 'space')), parts along dimension 0, may hold values 0 or 1
- void_mask: int32 [192, 16, 128], P(('design', 'space')), parts along dimension 0, may hold values 0 or 1
Outputs:
- smoothed: float32 [16, 3, 96, 16, 128], P(('design', 'case'), None, 'space'), parts along dimension 0
- new_density: float32 [192, 16, 128], P(('design', 'space')), parts along dimension 0
- ks_value: float32 [2], P('design'), parts along dimension 0
The draws below stay inside these ranges and needn't reach their ends.
There are 2 independent parts, one for each index of `design`. The reference program is written for one: setup_inputs(seed, part) draws one part's arguments, and reference() takes and returns one part's arrays. A program takes and returns all parts, laid end to end along the dimension named above; each array names one. Nothing has to cross between parts.
All inputs are finite; a program needn't handle non-finite values. No bound on the sum of `support_mask` or of `void_mask` on one device may be relied on, other than what follows from the above.
Results may differ from the reference program's by a relative error of at most 0.00002.
Values sent between devices are 32-bit elements; how exact they have to be, the bound alone decides.
A program may use at most 64 MiB of HBM per device.

```python
import math
import jax
import jax.numpy as jnp
from jax import lax

NY = 16
NZ = 128
CASES = 8
NX = 96


def draw_forces(key, part):
    key_scale, key_base = jax.random.split(jax.random.fold_in(key, 11))
    scales = jnp.exp(jax.random.uniform(key_scale, (CASES, 1, 1, 1, 1), jnp.float32, -0.7, 0.7))
    base = jnp.clip(jax.random.normal(key_base, (CASES, 3, NX, NY, NZ), jnp.float32), -4.0, 4.0)
    return scales * base


def plant(result, key, low, high):
    spot = [jax.random.randint(jax.random.fold_in(key, axis), (), 0, length) for axis, length in enumerate(result.shape)]
    main_axis = result.shape.index(max(result.shape))
    beside = spot[:main_axis] + [(spot[main_axis] + 1) % result.shape[main_axis]] + spot[main_axis + 1:]
    return result.at[tuple(spot)].set(low).at[tuple(beside)].set(high)


def levels(key, dims, cuts, low, top_value):
    gain, own = 1.0, jax.random.fold_in(key, 6)
    for position, blocks in cuts:
        heights = jnp.exp(jax.random.uniform(jax.random.fold_in(own, position), (blocks,), jnp.float32, low / len(cuts), top_value / len(cuts)))
        gain = gain * jnp.repeat(heights, dims[position] // blocks).reshape([-1 if axis == position else 1 for axis in range(len(dims))])
    return gain


def gaussian(stream_key, shape, scale, bound, pieces=(), held_as=jnp.bfloat16):
    result = jax.random.normal(stream_key, shape, jnp.float32) * scale
    if len(pieces) > 0:
        result = levels(stream_key, shape, pieces, -0.22, 0.18) * result
    return jnp.clip(result, min=-bound, max=bound).astype(held_as)


def setup_inputs(seed: int = 0, part: int = 0) -> dict:
    keys = jax.random.split(jax.random.key(seed), 6)
    part_splits = jax.random.split(jax.random.fold_in(keys[5], part), 6)
    return {
        "displacement": gaussian(part_splits[0], (CASES, 3, NX, NY, NZ), 0.5, 3.0, ((0, 2), (2, 8)), jnp.float32),
        "forces": draw_forces(jax.random.fold_in(jax.random.fold_in(keys[5], part), 71), part),
        "density": jnp.clip(0.1 + 0.9 * jax.random.uniform(part_splits[2], (NX, NY, NZ), jnp.float32) ** levels(part_splits[2], (NX, NY, NZ), ((0, 8),), -0.2, 0.2), 0.1, 1.0),
        "support_mask": plant((jax.random.randint(part_splits[3], (NX, NY, NZ), 0, 16) < 1).astype(jnp.int32), jax.random.fold_in(part_splits[3], 1), 0, 1),
        "void_mask": plant((jax.random.randint(part_splits[4], (NX, NY, NZ), 0, 8) < 1).astype(jnp.int32), jax.random.fold_in(part_splits[4], 1), 0, 1),
    }


STIFF_MIN = 0.001
DIAG_SHIFT = 0.5
KS_BETA = 8.0
MOVE_LIMIT = 0.2
DENSITY_MIN = 0.001
STEP_ONE = 1.0 / (1.15 + 0.85 * math.cos(math.pi / 4))
STEP_TWO = 1.0 / (1.15 - 0.85 * math.cos(math.pi / 4))


def pad_axis(values, axis, width):
    widths = [(0, 0)] * values.ndim
    widths[values.ndim + axis] = (width, width)
    return jnp.pad(values, widths)


def stencil(fields, cube):
    face_x = STIFF_MIN + 0.5 * (cube[:-1] + cube[1:])
    middle = cube[1:-1]
    cube_y = pad_axis(middle, -2, 1)
    face_y = STIFF_MIN + 0.5 * (cube_y[:, :-1] + cube_y[:, 1:])
    cube_z = pad_axis(middle, -1, 1)
    face_z = STIFF_MIN + 0.5 * (cube_z[:, :, :-1] + cube_z[:, :, 1:])
    centre = fields[..., 1:-1, :, :]
    padded_y = pad_axis(centre, -2, 1)
    padded_z = pad_axis(centre, -1, 1)
    fluxes = face_x[1:] * (centre - fields[..., 2:, :, :]) + face_x[:-1] * (centre - fields[..., :-2, :, :])
    fluxes = fluxes + face_y[:, 1:] * (centre - padded_y[..., 2:, :]) + face_y[:, :-1] * (centre - padded_y[..., :-2, :])
    fluxes = fluxes + face_z[:, :, 1:] * (centre - padded_z[..., 2:]) + face_z[:, :, :-1] * (centre - padded_z[..., :-2])
    diagonal = DIAG_SHIFT + face_x[1:] + face_x[:-1] + face_y[:, 1:] + face_y[:, :-1] + face_z[:, :, 1:] + face_z[:, :, :-1]
    return DIAG_SHIFT * centre + fluxes, diagonal


def smooth_sweep(fields, loads, cube, keep, factor):
    applied, diagonal = stencil(fields, cube)
    centre = fields[..., 1:-1, :, :]
    return keep * (centre + factor * (loads - applied) / diagonal)


def energy(extended, density):
    centre = extended[..., 1:-1, :, :]
    padded_y = pad_axis(centre, -2, 1)
    padded_z = pad_axis(centre, -1, 1)
    squares = (centre - extended[..., 2:, :, :]) ** 2 + (centre - extended[..., :-2, :, :]) ** 2
    squares = squares + (centre - padded_y[..., 2:, :]) ** 2 + (centre - padded_y[..., :-2, :]) ** 2
    squares = squares + (centre - padded_z[..., 2:]) ** 2 + (centre - padded_z[..., :-2]) ** 2
    return -1.5 * density * density * jnp.sum(squares, axis=-4)


def reference(displacement, forces, density, support_mask, void_mask):
    cube_pad = pad_axis(density ** 3, -3, 1)
    keep = (1 - support_mask).astype(jnp.float32)

    def one_case(pair):
        motion, loads = pair
        motion = smooth_sweep(pad_axis(motion, -3, 1), loads, cube_pad, keep, STEP_ONE)
        motion = smooth_sweep(pad_axis(motion, -3, 1), loads, cube_pad, keep, STEP_TWO)
        case_sens = energy(pad_axis(motion, -3, 1), density)
        return motion, case_sens, jnp.sum(loads * motion)

    smoothed, all_sens, compliance = lax.map(one_case, (displacement, forces))
    scores = KS_BETA * compliance / (3.0 * NX * NY * NZ)
    highest = jnp.max(scores)
    exponent = jnp.exp(scores - highest)
    denominator = jnp.sum(exponent)
    weights = exponent / denominator
    ks_value = (highest + jnp.log(denominator)) / KS_BETA
    combined = jnp.sum(weights[:, None, None, None] * all_sens, axis=0)
    product = density * combined
    padded = jnp.pad(product, 1)
    ones_pad = jnp.pad(jnp.ones_like(product), 1)
    neighbours = padded[2:, 1:-1, 1:-1] + padded[:-2, 1:-1, 1:-1] + padded[1:-1, 2:, 1:-1]
    neighbours = neighbours + padded[1:-1, :-2, 1:-1] + padded[1:-1, 1:-1, 2:] + padded[1:-1, 1:-1, :-2]
    counts = ones_pad[2:, 1:-1, 1:-1] + ones_pad[:-2, 1:-1, 1:-1] + ones_pad[1:-1, 2:, 1:-1]
    counts = counts + ones_pad[1:-1, :-2, 1:-1] + ones_pad[1:-1, 1:-1, 2:] + ones_pad[1:-1, 1:-1, :-2]
    filtered = (2.0 * product + neighbours) / (density * (2.0 + counts))
    scale = jnp.sum(-filtered) / (NX * NY * NZ) + 1e-6
    updated = jnp.clip(density + MOVE_LIMIT * (-filtered / scale - 1.0), DENSITY_MIN, 1.0)
    new_density = jnp.where(void_mask == 1, DENSITY_MIN, updated)
    return smoothed, new_density, ks_value.reshape(1)
```

```python
import functools
import math

import jax
import jax.numpy as jnp
from jax import lax
from jax.experimental import pallas as pl
from jax.experimental.pallas import tpu as pltpu
from jax.sharding import PartitionSpec as P

STIFF_MIN = 0.001
DIAG_SHIFT = 0.5
KS_BETA = 8.0
MOVE_LIMIT = 0.2
DENSITY_MIN = 0.001
STEP_ONE = 1.0 / (1.15 + 0.85 * math.cos(math.pi / 4))
STEP_TWO = 1.0 / (1.15 - 0.85 * math.cos(math.pi / 4))
F32 = jnp.float32
MESH = pl.DeviceIdType.MESH


def kernel(
    n_space, n_case,
    disp, forces, dens, sup, void,
    out, newd, ks,
    v, f, s1, s2, d, cube, inv, sup_v, void_v,
    kx, kyp, kym, kzp, kzm, keep, rdk, hsum, e, u, up,
    acc, gath,
    load_sem, dens_load, out_sem,
    send_sem, recv_sem, dsend, drecv, usend, urecv, gsend, grecv,
):
    cases, comps, planes, rows, lanes = disp.shape
    s = lax.axis_index("space")
    mine = lax.axis_index("case")
    members = n_space * n_case
    me = s * n_case + mine
    has_lo = s > 0
    has_hi = s < n_space - 1
    lo = jnp.maximum(s - 1, 0)
    hi = jnp.minimum(s + 1, n_space - 1)
    last = planes + 1

    barrier = pltpu.get_barrier_semaphore()

    def greet(step, carry):
        peer = lax.rem(me + step, members)
        pl.semaphore_signal(
            barrier, inc=1,
            device_id={"space": peer // n_case, "case": lax.rem(peer, n_case)},
            device_id_type=MESH,
        )
        return carry

    lax.fori_loop(1, members, greet, 0)

    own = pl.ds(1, planes)
    dens_loads = [
        pltpu.make_async_copy(dens, d.at[own], dens_load.at[0]),
        pltpu.make_async_copy(sup, sup_v, dens_load.at[1]),
        pltpu.make_async_copy(void, void_v, dens_load.at[2]),
    ]
    for copy in dens_loads:
        copy.start()

    def disp_load(c):
        return pltpu.make_async_copy(disp.at[c], v.at[c, :, own], load_sem.at[0, c])

    def force_load(c):
        return pltpu.make_async_copy(forces.at[c], f.at[c], load_sem.at[1, c])

    for c in range(cases):
        disp_load(c).start()
        force_load(c).start()

    @pl.when(s == 0)
    def _():
        zero = jnp.zeros((rows, lanes), F32)
        d[0] = zero
        u[0] = zero
        up[0] = zero
        for ref in (v, s1, s2):
            ref[:, :, 0] = jnp.zeros((cases, comps, rows, lanes), F32)

    @pl.when(s == n_space - 1)
    def _():
        zero = jnp.zeros((rows, lanes), F32)
        d[last] = zero
        u[last] = zero
        up[last] = zero
        for ref in (v, s1, s2):
            ref[:, :, last] = jnp.zeros((cases, comps, rows, lanes), F32)

    pl.semaphore_wait(barrier, members - 1)

    def remote(src, dst, ssem, rsem, peer):
        return pltpu.make_async_remote_copy(
            src_ref=src, dst_ref=dst, send_sem=ssem, recv_sem=rsem,
            device_id={"space": peer}, device_id_type=MESH,
        )

    def dens_up():
        return remote(dens.at[planes - 1], d.at[0], dsend.at[0], drecv.at[0], hi)

    def dens_down():
        return remote(dens.at[0], d.at[last], dsend.at[1], drecv.at[1], lo)

    bufs = (v, s1, s2)

    def face_up(stage, c):
        src = disp.at[c, :, planes - 1] if stage == 0 else bufs[stage].at[c, :, planes]
        return remote(
            src, bufs[stage].at[c, :, 0], send_sem.at[stage, c, 0], recv_sem.at[stage, c, 0], hi
        )

    def face_down(stage, c):
        src = disp.at[c, :, 0] if stage == 0 else bufs[stage].at[c, :, 1]
        return remote(
            src, bufs[stage].at[c, :, last], send_sem.at[stage, c, 1], recv_sem.at[stage, c, 1], lo
        )

    def send_faces(stage, c):
        @pl.when(has_hi)
        def _():
            face_up(stage, c).start()

        @pl.when(has_lo)
        def _():
            face_down(stage, c).start()

    def await_faces(stage, c):
        @pl.when(has_lo)
        def _():
            face_up(stage, c).wait_recv()

        @pl.when(has_hi)
        def _():
            face_down(stage, c).wait_recv()

    @pl.when(has_hi)
    def _():
        dens_up().start()

    @pl.when(has_lo)
    def _():
        dens_down().start()

    for c in range(cases):
        send_faces(0, c)

    y_id = lax.broadcasted_iota(jnp.int32, (rows, lanes), 0)
    z_id = lax.broadcasted_iota(jnp.int32, (rows, lanes), 1)
    y_first, y_last = y_id == 0, y_id == rows - 1
    z_first, z_last = z_id == 0, z_id == lanes - 1
    yz_count = (
        4.0 + 2.0 - y_first.astype(F32) - y_last.astype(F32)
        - z_first.astype(F32) - z_last.astype(F32)
    )

    def next_y(value):
        return pltpu.roll(value, rows - 1, value.ndim - 2)

    def prev_y(value):
        return pltpu.roll(value, 1, value.ndim - 2)

    def next_z(value):
        return pltpu.roll(value, lanes - 1, value.ndim - 1)

    def prev_z(value):
        return pltpu.roll(value, 1, value.ndim - 1)

    def cube_of(j):
        value = d[j]
        cube[j] = value * value * value

    total_planes = planes * n_space

    def inv_of(j):
        g = s * planes + j - 1
        x_count = (g > 0).astype(F32) + (g < total_planes - 1).astype(F32)
        inside = jnp.logical_and(g >= 0, g < total_planes).astype(F32)
        value = jnp.where(d[j] > 0, d[j], 1.0)
        inv[j] = inside / (value * (yz_count + x_count))

    def coefficients(j):
        here = cube[j]
        face_lo = STIFF_MIN + 0.5 * (cube[j - 1] + here)
        face_hi = STIFF_MIN + 0.5 * (here + cube[j + 1])
        kx[j - 1] = face_lo
        kx[j] = face_hi
        y_hi = STIFF_MIN + 0.5 * (here + jnp.where(y_last, 0.0, next_y(here)))
        y_lo = STIFF_MIN + 0.5 * (here + jnp.where(y_first, 0.0, prev_y(here)))
        z_hi = STIFF_MIN + 0.5 * (here + jnp.where(z_last, 0.0, next_z(here)))
        z_lo = STIFF_MIN + 0.5 * (here + jnp.where(z_first, 0.0, prev_z(here)))
        diagonal = DIAG_SHIFT + face_hi + face_lo + y_hi + y_lo + z_hi + z_lo
        kyp[j - 1] = jnp.where(y_last, 0.0, y_hi)
        kym[j - 1] = jnp.where(y_first, 0.0, y_lo)
        kzp[j - 1] = jnp.where(z_last, 0.0, z_hi)
        kzm[j - 1] = jnp.where(z_first, 0.0, z_lo)
        kept = (1 - sup_v[j - 1]).astype(F32)
        keep[j - 1] = kept
        rdk[j - 1] = kept / diagonal

    def around(value):
        return (
            jnp.where(y_last, 0.0, next_y(value)) + jnp.where(y_first, 0.0, prev_y(value))
            + jnp.where(z_last, 0.0, next_z(value)) + jnp.where(z_first, 0.0, prev_z(value))
        )

    def filter_sum(j):
        here = inv[j]
        total = 2.0 * here + inv[j - 1] + inv[j + 1] + around(here)
        hsum[j - 1] = 1.5 * cube[j] * total

    def loop(start, stop, fn, unroll=1):
        def step(i, carry):
            fn(i)
            return carry

        lax.fori_loop(start, stop, step, 0, unroll=unroll)

    for copy in dens_loads:
        copy.wait()
    loop(1, last, cube_of)
    loop(1, last, inv_of)
    loop(2, planes, coefficients)

    def sweep(src, dst, c, j, factor):
        centre = src[c, :, j]
        load = f[c, :, j - 1]
        total = load + kx[j - 1] * src[c, :, j - 1] + kx[j] * src[c, :, j + 1]
        total = total + kyp[j - 1] * next_y(centre) + kym[j - 1] * prev_y(centre)
        total = total + kzp[j - 1] * next_z(centre) + kzm[j - 1] * prev_z(centre)
        result = (keep[j - 1] * (1.0 - factor)) * centre + (rdk[j - 1] * factor) * total
        dst[c, :, j] = result
        return load, result

    def energy(c, j):
        centre = s2[c, :, j]
        low = centre - s2[c, :, j - 1]
        high = centre - s2[c, :, j + 1]
        y_hi = centre - jnp.where(y_last, 0.0, next_y(centre))
        y_lo = centre - jnp.where(y_first, 0.0, prev_y(centre))
        z_hi = centre - jnp.where(z_last, 0.0, next_z(centre))
        z_lo = centre - jnp.where(z_first, 0.0, prev_z(centre))
        squares = low * low + high * high + y_hi * y_hi + y_lo * y_lo + z_hi * z_hi + z_lo * z_lo
        value = jnp.sum(squares, axis=0)
        e[c, j - 1] = value
        return value * hsum[j - 1]

    def interior_one(c):
        disp_load(c).wait()
        force_load(c).wait()
        loop(2, planes, lambda j: sweep(v, s1, c, j, STEP_ONE), unroll=2)

    loop(0, cases, interior_one)

    @pl.when(has_lo)
    def _():
        dens_up().wait_recv()

    @pl.when(has_hi)
    def _():
        dens_down().wait_recv()

    cube_of(0)
    cube_of(last)
    inv_of(0)
    inv_of(last)
    coefficients(1)
    coefficients(planes)
    loop(1, last, filter_sum)

    zero = jnp.zeros((rows, lanes), F32)

    def stage_one(c):
        await_faces(0, c)
        sweep(v, s1, c, 1, STEP_ONE)
        sweep(v, s1, c, planes, STEP_ONE)
        send_faces(1, c)

        def step(j, total):
            load, result = sweep(s1, s2, c, j, STEP_TWO)
            return total + jnp.sum(load * result, axis=0)

        acc[0, c] = lax.fori_loop(2, planes, step, zero, unroll=2)

    loop(0, cases, stage_one)

    def out_copy(c):
        return pltpu.make_async_copy(s2.at[c, :, own], out.at[c], out_sem.at[c])

    def stage_two(c):
        await_faces(1, c)
        load, result = sweep(s1, s2, c, 1, STEP_TWO)
        total = acc[0, c] + jnp.sum(load * result, axis=0)
        load, result = sweep(s1, s2, c, planes, STEP_TWO)
        acc[0, c] = total + jnp.sum(load * result, axis=0)
        send_faces(2, c)
        out_copy(c).start()
        acc[1, c] = lax.fori_loop(
            2, planes, lambda j, total: total + energy(c, j), zero, unroll=2
        )

    loop(0, cases, stage_two)

    lane = lax.broadcasted_iota(jnp.int32, (1, lanes), 1)

    def gather_copy(which, peer):
        return pltpu.make_async_remote_copy(
            src_ref=gath.at[which, me], dst_ref=gath.at[which, me],
            send_sem=gsend.at[which], recv_sem=grecv.at[which],
            device_id={"space": peer // n_case, "case": lax.rem(peer, n_case)},
            device_id_type=MESH,
        )

    def gather_start(which):
        row = jnp.zeros((1, lanes), F32)
        for c in range(cases):
            part = jnp.sum(jnp.sum(acc[which, c], axis=0, keepdims=True), axis=1, keepdims=True)
            row = jnp.where(lane == mine * cases + c, part, row)
        gath[which, me] = row
        loop(1, members, lambda step: gather_copy(which, lax.rem(me + step, members)).start())

    def whole(which):
        return gath.at[which, pl.ds(0, members - 1)]

    def gather_wait(which):
        pltpu.make_async_copy(whole(which), whole(which), grecv.at[which]).wait()
        return jnp.sum(gath[which], axis=0)

    gather_start(0)

    def stage_three(c):
        await_faces(2, c)
        acc[1, c] = acc[1, c] + energy(c, 1) + energy(c, planes)

    loop(0, cases, stage_three)
    gather_start(1)

    cells = total_planes * rows * lanes
    valid = lane < cases * n_case
    scores = (KS_BETA / (3.0 * cells)) * gather_wait(0)
    top = jnp.max(jnp.where(valid, scores, -3.0e38), axis=1, keepdims=True)
    exponent = jnp.where(valid, jnp.exp(jnp.where(valid, scores - top, 0.0)), 0.0)
    total = jnp.sum(exponent, axis=1, keepdims=True)
    weights = exponent / total
    ks[0] = jnp.max((top + jnp.log(total)) / KS_BETA)
    picks = [
        jnp.sum(jnp.where(lane == mine * cases + c, weights, 0.0), axis=1, keepdims=True)
        for c in range(cases)
    ]

    def mix(j):
        value = picks[0] * e[0, j - 1]
        for c in range(1, cases):
            value = value + picks[c] * e[c, j - 1]
        u[j] = value

    mix(1)
    mix(planes)

    other = 1 - mine if n_case == 2 else lax.rem(mine + 1, n_case)

    def rim(dst, index, peer, case, src):
        return pltpu.make_async_remote_copy(
            src_ref=u.at[src], dst_ref=dst,
            send_sem=usend.at[index], recv_sem=urecv.at[index],
            device_id={"space": peer, "case": case}, device_id_type=MESH,
        )

    rims_up = [rim(u.at[0], 0, hi, mine, planes), rim(up.at[0], 1, hi, other, planes)]
    rims_down = [rim(u.at[last], 2, lo, mine, 1), rim(up.at[last], 3, lo, other, 1)]

    @pl.when(has_hi)
    def _():
        for copy in rims_up:
            copy.start()

    @pl.when(has_lo)
    def _():
        for copy in rims_down:
            copy.start()

    loop(2, planes, mix, unroll=2)
    across = rim(up.at[own], 4, s, other, own)
    across.start()
    across.wait_recv()

    @pl.when(has_lo)
    def _():
        for copy in rims_up:
            copy.wait_recv()

    @pl.when(has_hi)
    def _():
        for copy in rims_down:
            copy.wait_recv()

    def product(j):
        cube[j] = 1.5 * cube[j] * (u[j] + up[j])

    loop(0, last + 1, product, unroll=2)

    def filtered(j):
        here = cube[j]
        kx[j - 1] = inv[j] * (2.0 * here + cube[j - 1] + cube[j + 1] + around(here))

    loop(1, last, filtered, unroll=2)

    sums = gather_wait(1)
    scale = jnp.sum(weights * jnp.where(valid, sums, 0.0), axis=1, keepdims=True) / cells + 1e-06

    def update(j):
        value = d[j] + MOVE_LIMIT * (kx[j - 1] / scale - 1.0)
        value = jnp.minimum(jnp.maximum(value, DENSITY_MIN), 1.0)
        newd[j - 1] = jnp.where(void_v[j - 1] == 1, DENSITY_MIN, value)

    loop(1, last, update, unroll=2)

    @pl.when(has_hi)
    def _():
        dens_up().wait_send()
        for copy in rims_up:
            copy.wait_send()
        for stage in range(3):
            loop(0, cases, lambda c: face_up(stage, c).wait_send())

    @pl.when(has_lo)
    def _():
        dens_down().wait_send()
        for copy in rims_down:
            copy.wait_send()
        for stage in range(3):
            loop(0, cases, lambda c: face_down(stage, c).wait_send())

    across.wait_send()
    for which in range(2):
        pltpu.make_async_copy(whole(which), whole(which), gsend.at[which]).wait()
    loop(0, cases, lambda c: out_copy(c).wait())


def solution(mesh):
    n_space, n_case = mesh.shape["space"], mesh.shape["case"]
    members = n_space * n_case

    def body(displacement, forces, density, support_mask, void_mask):
        cases, comps, planes, rows, lanes = displacement.shape
        padded = (cases, comps, planes + 2, rows, lanes)
        slab = (planes, rows, lanes)
        thick = (planes + 2, rows, lanes)
        any_space = pl.BlockSpec(memory_space=pl.ANY)
        vmem = lambda shape, dtype=F32: pltpu.VMEM(shape, dtype)
        dma = pltpu.SemaphoreType.DMA
        return pl.pallas_call(
            functools.partial(kernel, n_space, n_case),
            out_shape=(
                jax.ShapeDtypeStruct(displacement.shape, F32),
                jax.ShapeDtypeStruct(density.shape, F32),
                jax.ShapeDtypeStruct((1,), F32),
            ),
            in_specs=[any_space] * 5,
            out_specs=(
                any_space,
                pl.BlockSpec(memory_space=pltpu.VMEM),
                pl.BlockSpec(memory_space=pltpu.SMEM),
            ),
            scratch_shapes=[
                vmem(padded), vmem(displacement.shape), vmem(padded), vmem(padded),
                vmem(thick), vmem(thick), vmem(thick),
                vmem(slab, jnp.int32), vmem(slab, jnp.int32),
                vmem((planes + 1, rows, lanes)),
                vmem(slab), vmem(slab), vmem(slab), vmem(slab), vmem(slab), vmem(slab),
                vmem(slab),
                vmem((cases,) + slab), vmem(thick), vmem(thick),
                vmem((2, cases, rows, lanes)),
                vmem((2, members, 1, lanes)),
                dma((2, cases)), dma((3,)), dma((cases,)),
                dma((3, cases, 2)), dma((3, cases, 2)), dma((2,)), dma((2,)),
                dma((5,)), dma((5,)), dma((2,)), dma((2,)),
            ],
            compiler_params=pltpu.CompilerParams(collective_id=0, has_side_effects=True),
        )(displacement, forces, density, support_mask, void_mask)

    return jax.shard_map(
        body,
        mesh=mesh,
        in_specs=(
            P(("design", "case"), None, "space", None, None),
            P(("design", "case"), None, "space", None, None),
            P(("design", "space"), None, None),
            P(("design", "space"), None, None),
            P(("design", "space"), None, None),
        ),
        out_specs=(
            P(("design", "case"), None, "space", None, None),
            P(("design", "space"), None, None),
            P("design"),
        ),
        check_vma=False,
    )
```

```python
import functools
import math

import jax
import jax.numpy as jnp
from jax import lax
from jax.experimental import pallas as pl
from jax.experimental.pallas import tpu as pltpu
from jax.sharding import PartitionSpec as P

STIFF_MIN = 0.001
DIAG_SHIFT = 0.5
KS_BETA = 8.0
MOVE_LIMIT = 0.2
DENSITY_MIN = 0.001
STEP_ONE = 1.0 / (1.15 + 0.85 * math.cos(math.pi / 4))
STEP_TWO = 1.0 / (1.15 - 0.85 * math.cos(math.pi / 4))
F32 = jnp.float32
MESH = pl.DeviceIdType.MESH


def kernel(
    n_space, n_case,
    disp, forces, dens, sup, void,
    out, newd, ks,
    v, f, s1, s2, d, cube, inv, sup_v, void_v,
    kx, kyp, kym, kzp, kzm, keep, rdk, hsum, e, u, up,
    acc, gath,
    load_sem, dens_load, out_sem,
    send_sem, recv_sem, dsend, drecv, usend, urecv, gsend, grecv, known,
):
    cases, comps, planes, rows, lanes = disp.shape
    s = lax.axis_index("space")
    mine = lax.axis_index("case")
    members = n_space * n_case
    me = s * n_case + mine
    has_lo = s > 0
    has_hi = s < n_space - 1
    lo = jnp.maximum(s - 1, 0)
    hi = jnp.minimum(s + 1, n_space - 1)
    last = planes + 1

    other = 1 - mine if n_case == 2 else lax.rem(mine + 1, n_case)

    barrier = pltpu.get_barrier_semaphore()

    def greet(sem, distance):
        @pl.when(s >= distance)
        def _():
            pl.semaphore_signal(
                sem, inc=1, device_id={"space": jnp.maximum(s - distance, 0)}, device_id_type=MESH
            )

        @pl.when(s < n_space - distance)
        def _():
            pl.semaphore_signal(
                sem, inc=1, device_id={"space": jnp.minimum(s + distance, n_space - 1)},
                device_id_type=MESH,
            )

    def greeted(distance):
        return (s >= distance).astype(jnp.int32) + (s < n_space - distance).astype(jnp.int32)

    greet(barrier, 1)
    for step in range(1, n_case):
        pl.semaphore_signal(
            barrier, inc=1, device_id={"case": lax.rem(mine + step, n_case)}, device_id_type=MESH
        )

    distances = [1]
    while distances[-1] < n_space:
        distances.append(2 * distances[-1])
    distances = [1] + distances[:-1] if n_space > 1 else []
    distances = distances[1:]

    def widen_start(k):
        if k < len(distances):
            greet(known.at[k], distances[k])

    def widen_wait(k):
        if k < len(distances):
            pl.semaphore_wait(known.at[k], greeted(distances[k]))

    own = pl.ds(1, planes)
    dens_loads = [
        pltpu.make_async_copy(dens, d.at[own], dens_load.at[0]),
        pltpu.make_async_copy(sup, sup_v, dens_load.at[1]),
        pltpu.make_async_copy(void, void_v, dens_load.at[2]),
    ]
    for copy in dens_loads:
        copy.start()

    def disp_load(c):
        return pltpu.make_async_copy(disp.at[c], v.at[c, :, own], load_sem.at[0, c])

    def force_load(c):
        return pltpu.make_async_copy(forces.at[c], f.at[c], load_sem.at[1, c])

    for c in range(cases):
        disp_load(c).start()
        force_load(c).start()

    @pl.when(s == 0)
    def _():
        zero = jnp.zeros((rows, lanes), F32)
        d[0] = zero
        u[0] = zero
        up[0] = zero
        for ref in (v, s1, s2):
            ref[:, :, 0] = jnp.zeros((cases, comps, rows, lanes), F32)

    @pl.when(s == n_space - 1)
    def _():
        zero = jnp.zeros((rows, lanes), F32)
        d[last] = zero
        u[last] = zero
        up[last] = zero
        for ref in (v, s1, s2):
            ref[:, :, last] = jnp.zeros((cases, comps, rows, lanes), F32)

    pl.semaphore_wait(barrier, greeted(1) + (n_case - 1))

    def remote(src, dst, ssem, rsem, peer):
        return pltpu.make_async_remote_copy(
            src_ref=src, dst_ref=dst, send_sem=ssem, recv_sem=rsem,
            device_id={"space": peer}, device_id_type=MESH,
        )

    def dens_up():
        return remote(dens.at[planes - 1], d.at[0], dsend.at[0], drecv.at[0], hi)

    def dens_down():
        return remote(dens.at[0], d.at[last], dsend.at[1], drecv.at[1], lo)

    bufs = (v, s1, s2)

    def face_up(stage, c):
        src = disp.at[c, :, planes - 1] if stage == 0 else bufs[stage].at[c, :, planes]
        return remote(
            src, bufs[stage].at[c, :, 0], send_sem.at[stage, c, 0], recv_sem.at[stage, c, 0], hi
        )

    def face_down(stage, c):
        src = disp.at[c, :, 0] if stage == 0 else bufs[stage].at[c, :, 1]
        return remote(
            src, bufs[stage].at[c, :, last], send_sem.at[stage, c, 1], recv_sem.at[stage, c, 1], lo
        )

    def send_faces(stage, c):
        @pl.when(has_hi)
        def _():
            face_up(stage, c).start()

        @pl.when(has_lo)
        def _():
            face_down(stage, c).start()

    def await_faces(stage, c):
        @pl.when(has_lo)
        def _():
            face_up(stage, c).wait_recv()

        @pl.when(has_hi)
        def _():
            face_down(stage, c).wait_recv()

    @pl.when(has_hi)
    def _():
        dens_up().start()

    @pl.when(has_lo)
    def _():
        dens_down().start()

    for c in range(cases):
        send_faces(0, c)
    widen_start(0)

    y_id = lax.broadcasted_iota(jnp.int32, (rows, lanes), 0)
    z_id = lax.broadcasted_iota(jnp.int32, (rows, lanes), 1)
    y_first, y_last = y_id == 0, y_id == rows - 1
    z_first, z_last = z_id == 0, z_id == lanes - 1
    yz_count = (
        4.0 + 2.0 - y_first.astype(F32) - y_last.astype(F32)
        - z_first.astype(F32) - z_last.astype(F32)
    )

    def next_y(value):
        return pltpu.roll(value, rows - 1, value.ndim - 2)

    def prev_y(value):
        return pltpu.roll(value, 1, value.ndim - 2)

    def next_z(value):
        return pltpu.roll(value, lanes - 1, value.ndim - 1)

    def prev_z(value):
        return pltpu.roll(value, 1, value.ndim - 1)

    total_planes = planes * n_space

    def cube_of(j, n=1):
        value = d[pl.ds(j, n)]
        cube[pl.ds(j, n)] = value * value * value

    def inv_of(j, n=1):
        g = s * planes + j - 1 + lax.broadcasted_iota(jnp.int32, (n, rows, lanes), 0)
        x_count = (g > 0).astype(F32) + (g < total_planes - 1).astype(F32)
        inside = jnp.logical_and(g >= 0, g < total_planes)
        value = jnp.where(inside, d[pl.ds(j, n)], 1.0)
        inv[pl.ds(j, n)] = jnp.where(inside, 1.0 / (value * (yz_count + x_count)), 0.0)

    def coefficients(j, n=1):
        at = pl.ds(j - 1, n)
        here = cube[pl.ds(j, n)]
        face_lo = STIFF_MIN + 0.5 * (cube[at] + here)
        face_hi = STIFF_MIN + 0.5 * (here + cube[pl.ds(j + 1, n)])
        y_hi = STIFF_MIN + 0.5 * (here + jnp.where(y_last, 0.0, next_y(here)))
        y_lo = STIFF_MIN + 0.5 * (here + jnp.where(y_first, 0.0, prev_y(here)))
        z_hi = STIFF_MIN + 0.5 * (here + jnp.where(z_last, 0.0, next_z(here)))
        z_lo = STIFF_MIN + 0.5 * (here + jnp.where(z_first, 0.0, prev_z(here)))
        kept = (1 - sup_v[at]).astype(F32)
        diagonal = DIAG_SHIFT + face_hi + face_lo + y_hi + y_lo + z_hi + z_lo
        scaled = kept / diagonal
        kx[at] = face_lo
        kx[pl.ds(j, n)] = face_hi
        kyp[at] = jnp.where(y_last, 0.0, y_hi)
        kym[at] = jnp.where(y_first, 0.0, y_lo)
        kzp[at] = jnp.where(z_last, 0.0, z_hi)
        kzm[at] = jnp.where(z_first, 0.0, z_lo)
        keep[at] = kept
        rdk[at] = scaled

    def around(value):
        return (
            jnp.where(y_last, 0.0, next_y(value)) + jnp.where(y_first, 0.0, prev_y(value))
            + jnp.where(z_last, 0.0, next_z(value)) + jnp.where(z_first, 0.0, prev_z(value))
        )

    def filter_sum(j, n=1):
        here = inv[pl.ds(j, n)]
        total = 2.0 * here + inv[pl.ds(j - 1, n)] + inv[pl.ds(j + 1, n)] + around(here)
        hsum[pl.ds(j - 1, n)] = 1.5 * cube[pl.ds(j, n)] * total

    def loop(start, stop, fn, unroll=1):
        def step(i, carry):
            fn(i)
            return carry

        lax.fori_loop(start, stop, step, 0, unroll=unroll)

    def blocks(start, stop, size):
        return [(j, min(size, stop - j)) for j in range(start, stop, size)]

    inner = blocks(2, planes, 2)

    for copy in dens_loads:
        copy.wait()
    for j, n in blocks(1, last, 2):
        cube_of(j, n)
    for j, n in inner:
        coefficients(j, n)

    def sweep(src, dst, c, j, n, factor):
        at = pl.ds(j - 1, n)
        centre = src[c, :, pl.ds(j, n)]
        load = f[c, :, at]
        total = load + kx[at] * src[c, :, at] + kx[pl.ds(j, n)] * src[c, :, pl.ds(j + 1, n)]
        total = total + kyp[at] * next_y(centre) + kym[at] * prev_y(centre)
        total = total + kzp[at] * next_z(centre) + kzm[at] * prev_z(centre)
        result = (keep[at] * (1.0 - factor)) * centre + (rdk[at] * factor) * total
        dst[c, :, pl.ds(j, n)] = result
        return jnp.sum(jnp.sum(load * result, axis=0), axis=0)

    def energy(c, j, n):
        centre = s2[c, :, pl.ds(j, n)]
        low = centre - s2[c, :, pl.ds(j - 1, n)]
        high = centre - s2[c, :, pl.ds(j + 1, n)]
        y_hi = centre - jnp.where(y_last, 0.0, next_y(centre))
        y_lo = centre - jnp.where(y_first, 0.0, prev_y(centre))
        z_hi = centre - jnp.where(z_last, 0.0, next_z(centre))
        z_lo = centre - jnp.where(z_first, 0.0, prev_z(centre))
        squares = low * low + high * high + y_hi * y_hi + y_lo * y_lo + z_hi * z_hi + z_lo * z_lo
        value = jnp.sum(squares, axis=0)
        e[c, pl.ds(j - 1, n)] = value
        return jnp.sum(value * hsum[pl.ds(j - 1, n)], axis=0)

    def interior_one(c):
        disp_load(c).wait()
        force_load(c).wait()
        for j, n in inner:
            sweep(v, s1, c, j, n, STEP_ONE)

    loop(0, cases, interior_one)
    widen_wait(0)
    widen_start(1)

    @pl.when(has_lo)
    def _():
        dens_up().wait_recv()

    @pl.when(has_hi)
    def _():
        dens_down().wait_recv()

    cube_of(0)
    cube_of(last)
    coefficients(1)
    coefficients(planes)

    for c in range(cases):
        await_faces(0, c)
        sweep(v, s1, c, 1, 1, STEP_ONE)
        sweep(v, s1, c, planes, 1, STEP_ONE)
        send_faces(1, c)

    widen_wait(1)
    widen_start(2)
    for j, n in blocks(0, last + 1, 2):
        inv_of(j, n)
    for j, n in blocks(1, last, 2):
        filter_sum(j, n)

    def interior_two(c):
        acc[0, c] = sum(sweep(s1, s2, c, j, n, STEP_TWO) for j, n in inner)

    loop(0, cases, interior_two)

    def out_copy(c):
        return pltpu.make_async_copy(s2.at[c, :, own], out.at[c], out_sem.at[c])

    for c in range(cases):
        await_faces(1, c)
        part = sweep(s1, s2, c, 1, 1, STEP_TWO)
        acc[0, c] = acc[0, c] + part + sweep(s1, s2, c, planes, 1, STEP_TWO)
        send_faces(2, c)
        out_copy(c).start()

    lane = lax.broadcasted_iota(jnp.int32, (1, lanes), 1)

    def gather_copy(which, peer):
        return pltpu.make_async_remote_copy(
            src_ref=gath.at[which, me], dst_ref=gath.at[which, me],
            send_sem=gsend.at[which], recv_sem=grecv.at[which],
            device_id={"space": peer // n_case, "case": lax.rem(peer, n_case)},
            device_id_type=MESH,
        )

    def gather_start(which):
        row = jnp.zeros((1, lanes), F32)
        for c in range(cases):
            part = jnp.sum(jnp.sum(acc[which, c], axis=0, keepdims=True), axis=1, keepdims=True)
            row = jnp.where(lane == mine * cases + c, part, row)
        gath[which, me] = row
        loop(1, members, lambda step: gather_copy(which, lax.rem(me + step, members)).start())

    def whole(which):
        return gath.at[which, pl.ds(0, members - 1)]

    def gather_wait(which):
        pltpu.make_async_copy(whole(which), whole(which), grecv.at[which]).wait()
        return jnp.sum(gath[which], axis=0)

    for k in range(2, len(distances)):
        if k > 2:
            widen_start(k)
        widen_wait(k)
    gather_start(0)

    def interior_three(c):
        acc[1, c] = sum(energy(c, j, n) for j, n in inner)

    loop(0, cases, interior_three)

    for c in range(cases):
        await_faces(2, c)
        acc[1, c] = acc[1, c] + energy(c, 1, 1) + energy(c, planes, 1)

    gather_start(1)

    cells = total_planes * rows * lanes
    valid = lane < cases * n_case
    scores = (KS_BETA / (3.0 * cells)) * gather_wait(0)
    top = jnp.max(jnp.where(valid, scores, -3.0e38), axis=1, keepdims=True)
    exponent = jnp.where(valid, jnp.exp(jnp.where(valid, scores - top, 0.0)), 0.0)
    total = jnp.sum(exponent, axis=1, keepdims=True)
    weights = exponent / total
    ks[0] = jnp.max((top + jnp.log(total)) / KS_BETA)
    picks = [
        jnp.sum(jnp.where(lane == mine * cases + c, weights, 0.0), axis=1, keepdims=True)
        for c in range(cases)
    ]

    def mix(j, n=1):
        at = pl.ds(j - 1, n)
        value = picks[0] * e[0, at]
        for c in range(1, cases):
            value = value + picks[c] * e[c, at]
        u[pl.ds(j, n)] = value

    mix(1)
    mix(planes)

    def rim(dst, index, peer, case, src):
        return pltpu.make_async_remote_copy(
            src_ref=u.at[src], dst_ref=dst,
            send_sem=usend.at[index], recv_sem=urecv.at[index],
            device_id={"space": peer, "case": case}, device_id_type=MESH,
        )

    rims_up = [rim(u.at[0], 0, hi, mine, planes), rim(up.at[0], 1, hi, other, planes)]
    rims_down = [rim(u.at[last], 2, lo, mine, 1), rim(up.at[last], 3, lo, other, 1)]

    @pl.when(has_hi)
    def _():
        for copy in rims_up:
            copy.start()

    @pl.when(has_lo)
    def _():
        for copy in rims_down:
            copy.start()

    for j, n in inner:
        mix(j, n)
    across = rim(up.at[own], 4, s, other, own)
    across.start()
    across.wait_recv()

    @pl.when(has_lo)
    def _():
        for copy in rims_up:
            copy.wait_recv()

    @pl.when(has_hi)
    def _():
        for copy in rims_down:
            copy.wait_recv()

    for j, n in blocks(0, last + 1, 2):
        at = pl.ds(j, n)
        cube[at] = 1.5 * cube[at] * (u[at] + up[at])

    for j, n in blocks(1, last, 2):
        here = cube[pl.ds(j, n)]
        beside = cube[pl.ds(j - 1, n)] + cube[pl.ds(j + 1, n)]
        kx[pl.ds(j - 1, n)] = inv[pl.ds(j, n)] * (2.0 * here + beside + around(here))

    sums = gather_wait(1)
    scale = jnp.sum(weights * jnp.where(valid, sums, 0.0), axis=1, keepdims=True) / cells + 1e-06
    gain = MOVE_LIMIT / scale

    for j, n in blocks(1, last, 2):
        at = pl.ds(j - 1, n)
        value = d[pl.ds(j, n)] + (kx[at] * gain - MOVE_LIMIT)
        value = jnp.minimum(jnp.maximum(value, DENSITY_MIN), 1.0)
        newd[at] = jnp.where(void_v[at] == 1, DENSITY_MIN, value)

    @pl.when(has_hi)
    def _():
        dens_up().wait_send()
        for copy in rims_up:
            copy.wait_send()
        for stage in range(3):
            loop(0, cases, lambda c: face_up(stage, c).wait_send())

    @pl.when(has_lo)
    def _():
        dens_down().wait_send()
        for copy in rims_down:
            copy.wait_send()
        for stage in range(3):
            loop(0, cases, lambda c: face_down(stage, c).wait_send())

    across.wait_send()
    for which in range(2):
        pltpu.make_async_copy(whole(which), whole(which), gsend.at[which]).wait()
    loop(0, cases, lambda c: out_copy(c).wait())


def solution(mesh):
    n_space, n_case = mesh.shape["space"], mesh.shape["case"]
    members = n_space * n_case

    def body(displacement, forces, density, support_mask, void_mask):
        cases, comps, planes, rows, lanes = displacement.shape
        padded = (cases, comps, planes + 2, rows, lanes)
        slab = (planes, rows, lanes)
        thick = (planes + 2, rows, lanes)
        any_space = pl.BlockSpec(memory_space=pl.ANY)
        vmem = lambda shape, dtype=F32: pltpu.VMEM(shape, dtype)
        dma = pltpu.SemaphoreType.DMA
        return pl.pallas_call(
            functools.partial(kernel, n_space, n_case),
            out_shape=(
                jax.ShapeDtypeStruct(displacement.shape, F32),
                jax.ShapeDtypeStruct(density.shape, F32),
                jax.ShapeDtypeStruct((1,), F32),
            ),
            in_specs=[any_space] * 5,
            out_specs=(
                any_space,
                pl.BlockSpec(memory_space=pltpu.VMEM),
                pl.BlockSpec(memory_space=pltpu.SMEM),
            ),
            scratch_shapes=[
                vmem(padded), vmem(displacement.shape), vmem(padded), vmem(padded),
                vmem(thick), vmem(thick), vmem(thick),
                vmem(slab, jnp.int32), vmem(slab, jnp.int32),
                vmem((planes + 1, rows, lanes)),
                vmem(slab), vmem(slab), vmem(slab), vmem(slab), vmem(slab), vmem(slab),
                vmem(slab),
                vmem((cases,) + slab), vmem(thick), vmem(thick),
                vmem((2, cases, rows, lanes)),
                vmem((2, members, 1, lanes)),
                dma((2, cases)), dma((3,)), dma((cases,)),
                dma((3, cases, 2)), dma((3, cases, 2)), dma((2,)), dma((2,)),
                dma((5,)), dma((5,)), dma((2,)), dma((2,)),
                pltpu.SemaphoreType.REGULAR((8,)),
            ],
            compiler_params=pltpu.CompilerParams(collective_id=0, has_side_effects=True),
        )(displacement, forces, density, support_mask, void_mask)

    return jax.shard_map(
        body,
        mesh=mesh,
        in_specs=(
            P(("design", "case"), None, "space", None, None),
            P(("design", "case"), None, "space", None, None),
            P(("design", "space"), None, None),
            P(("design", "space"), None, None),
            P(("design", "space"), None, None),
        ),
        out_specs=(
            P(("design", "case"), None, "space", None, None),
            P(("design", "space"), None, None),
            P("design"),
        ),
        check_vma=False,
    )
```
